1024 devices in a mesh: dp: 16 (over x, core), expert: 64 (over z, y).
Axes of the slice: x: 8, y: 8, z: 8, core: 2. Of those that a mesh axis runs over, the one named last changes fastest.
Arguments:
- out_grad: bfloat16 [8192, 4096], P('expert', 'dp'), may hold values from -6 to 6
- layer_input: bfloat16 [8192, 4096], P('expert', 'dp'), may hold values from -0.59765625 to 0.59765625
- expert_ids: int32 [8192, 8], P('expert'), may hold values from 0 to 63, as said below
- selected_logits: float32 [8192, 8], P('expert'), may hold values from -6 to 6
- saved_hidden: bfloat16 [64, 64, 32, 768], P(None, 'expert'), may hold values from -6 to 6
- saved_output: bfloat16 [64, 64, 32, 4096], P(None, 'expert', None, 'dp'), may hold values from -0.375 to 0.375
- down_weight: bfloat16 [64, 4096, 768], P('expert', 'dp'), may hold values from -0.21875 to 0.21875
Outputs:
- hidden_grad: bfloat16 [64, 64, 32, 768], P(None, 'expert', 'dp')
- down_grad: float32 [64, 4096, 768], P('expert', 'dp')
- logit_grad: float32 [8192, 8], P('expert')
- router_grad: float32 [64, 4096], P('expert', 'dp')
The draws below stay inside these ranges and needn't reach their ends.
Inputs may be any that keep to these rules, and one draw needn't show every extreme that they name: `expert_ids`: each row names 8 different experts. In the rows of one device no expert is named more than 32 times, and some experts are named exactly 32 times by the rows of every device.
All inputs are finite; a program needn't handle non-finite values.
Results may differ from the reference program's by a relative error of at most 0.0057.
Values may be sent and summed in bfloat16 or wider, within the bound.
No kernel may reach another device: no remote copies, remote signals or barrier semaphores. Data moves between devices by JAX's collectives and lax.ppermute only.
A program may use at most 64 MiB of HBM per device.

```python
import jax
import jax.numpy as jnp
from jax import lax

D = 4096
FF = 768
EXPERTS = 64
TOP = 8
TOK_DEV = 128
CS = 32
TOKENS = 8192
N_EXPERT = 64


hot_count = 4


def draw_expert_ids(key, part):
    slots_dev = TOK_DEV * TOP
    blocks = TOKENS // TOK_DEV
    hot_order = jax.random.permutation(jax.random.fold_in(key, 101), EXPERTS)
    is_hot = jnp.zeros((EXPERTS,), jnp.int32).at[hot_order[:hot_count]].set(1) > 0
    others = jnp.logical_not(is_hot)
    other_count = EXPERTS - hot_count
    remaining = slots_dev - hot_count * CS
    base = remaining // other_count
    spare = remaining % other_count
    swing = max(0, min(base, CS - base - 1))

    def one_block(block_index):
        block_key = jax.random.fold_in(key, block_index + 1000)
        first_key, second_key, third_key = jax.random.split(block_key, 3)
        priority = jax.random.permutation(first_key, EXPERTS)
        beaten = jnp.logical_and(others[None, :], priority[None, :] < priority[:, None])
        rank_other = jnp.sum(beaten.astype(jnp.int32), axis=1)
        shifts = jax.random.randint(second_key, (EXPERTS,), 0, swing + 1)
        amount = shifts[rank_other // 2]
        paired = rank_other < other_count // 2 * 2
        sign = jnp.where(rank_other % 2 == 0, 1, -1)
        other_counts = base + (rank_other < spare).astype(jnp.int32) + jnp.where(paired, sign * amount, 0)
        counts = jnp.where(is_hot, CS, other_counts).astype(jnp.int32)
        dealt = jax.random.permutation(third_key, EXPERTS)
        running = jnp.cumsum(counts[dealt])
        entries = jnp.arange(slots_dev, dtype=jnp.int32)
        where_in = jnp.sum((running[None, :] <= entries[:, None]).astype(jnp.int32), axis=1)
        chosen = dealt[where_in].astype(jnp.int32)
        return chosen.reshape(TOP, TOK_DEV).T
    table = jax.vmap(one_block)(jnp.arange(blocks, dtype=jnp.int32))
    return table.reshape(TOKENS, TOP).astype(jnp.int32)


def levels(rng, dims, shards, least, largest):
    def one(dim, parts):
        draws = jax.random.uniform(jax.random.fold_in(jax.random.fold_in(rng, 6), dim), (parts,), jnp.float32, least / len(shards), largest / len(shards))
        return jnp.repeat(jnp.exp(draws), dims[dim] // parts).reshape((-1,) + (1,) * (len(dims) - dim - 1))

    gain = one(*shards[0])
    for cut in shards[1:]:
        gain = gain * one(*cut)
    return gain


def scatter_about(stream_key, extent, deviation, reach, shards=(), kind=jnp.bfloat16):
    gain = levels(stream_key, extent, shards, -0.22, 0.18) if shards else 1.0
    drawn = jax.random.normal(stream_key, extent, jnp.float32) * deviation * gain
    return jnp.minimum(jnp.maximum(drawn, -reach), reach).astype(kind)


def setup_inputs(seed: int = 0) -> dict:
    seeds = jax.random.split(jax.random.key(seed), 8)
    out_grad = scatter_about(seeds[0], (TOKENS, D), 1.0, 6.0, ((0, 64), (1, 16)))
    layer_input = scatter_about(seeds[1], (TOKENS, D), 0.1, 0.59765625, ((0, 64), (1, 16)))
    expert_ids = draw_expert_ids(jax.random.fold_in(seeds[7], 71), 0)
    selected_logits = scatter_about(seeds[3], (TOKENS, TOP), 1.5, 6.0, ((0, 64),), jnp.float32)
    saved_hidden = scatter_about(seeds[4], (N_EXPERT, EXPERTS, CS, FF), 1.0, 6.0, ((1, 64),))
    saved_output = scatter_about(seeds[5], (N_EXPERT, EXPERTS, CS, D), 0.0625, 0.375, ((1, 64), (3, 16)))
    down_weight = scatter_about(seeds[6], (EXPERTS, D, FF), FF ** -0.5, 0.21875, ((0, 64), (1, 16)))
    return dict(out_grad=out_grad, layer_input=layer_input, expert_ids=expert_ids, selected_logits=selected_logits, saved_hidden=saved_hidden, saved_output=saved_output, down_weight=down_weight)


def slot_block(row):
    same = row[:, None] == row[None, :]
    positions = jnp.arange(row.shape[0], dtype=jnp.int32)
    earlier = positions[None, :] < positions[:, None]
    return jnp.sum(jnp.logical_and(same, earlier), axis=1).astype(jnp.int32)


def reference(out_grad, layer_input, expert_ids, selected_logits, saved_hidden, saved_output, down_weight):
    slots_dev = TOK_DEV * TOP
    routed = expert_ids.reshape(N_EXPERT, slots_dev)
    slot_index = lax.map(slot_block, routed)
    raised = jnp.exp(selected_logits)
    gating = raised / jnp.sum(raised, axis=-1, keepdims=True)
    gate_rounded = gating.astype(jnp.bfloat16)
    source = jnp.broadcast_to(jnp.arange(N_EXPERT, dtype=jnp.int32)[:, None], (N_EXPERT, slots_dev))
    numbers = jnp.broadcast_to(jnp.arange(slots_dev, dtype=jnp.int32)[None, :] + 1, (N_EXPERT, slots_dev))
    pick_of = jnp.zeros((N_EXPERT, EXPERTS, CS), jnp.int32).at[source, routed, slot_index].set(numbers)
    live = pick_of > 0
    pick_flat = jnp.maximum(pick_of - 1, 0).astype(jnp.int32)
    token_global = (jnp.arange(N_EXPERT, dtype=jnp.int32)[:, None, None] * TOK_DEV + pick_flat // TOP).astype(jnp.int32)
    gate_flat = gate_rounded.reshape(N_EXPERT, slots_dev)
    gate_slot = jnp.take_along_axis(gate_flat, pick_flat.reshape(N_EXPERT, EXPERTS * CS), axis=1).reshape(N_EXPERT, EXPERTS, CS)
    gate_slot = jnp.where(live, gate_slot, jnp.zeros((), jnp.bfloat16))

    def per_expert(expert_index):
        tokens_here = token_global[:, expert_index]
        rows = out_grad[tokens_here]
        gates = gate_slot[:, expert_index]
        scaled = (gates[..., None].astype(jnp.float32) * rows.astype(jnp.float32)).astype(jnp.bfloat16)
        scaled_f = scaled.astype(jnp.float32)
        weight = down_weight[expert_index].astype(jnp.float32)
        hidden = saved_hidden[:, expert_index].astype(jnp.float32)
        delta_hidden = jnp.einsum('scd,df->scf', scaled_f, weight).astype(jnp.bfloat16)
        grad_weight = jnp.einsum('scd,scf->df', scaled_f, hidden)
        outputs = saved_output[:, expert_index].astype(jnp.float32)
        delta = jnp.sum(rows.astype(jnp.float32) * outputs, axis=-1)
        return delta_hidden, grad_weight, delta

    delta_all, down_grad, delta_slots = lax.map(per_expert, jnp.arange(EXPERTS, dtype=jnp.int32))
    hidden_grad = jnp.transpose(delta_all, (1, 0, 2, 3))
    delta_by = jnp.transpose(delta_slots, (1, 0, 2))
    gate_delta = delta_by[source, routed, slot_index].reshape(TOKENS, TOP)
    logit_grad = gating * (gate_delta - jnp.sum(gating * gate_delta, axis=-1, keepdims=True))
    onehot = (expert_ids[:, :, None] == jnp.arange(EXPERTS, dtype=jnp.int32)[None, None, :]).astype(jnp.float32)
    weights_by_expert = jnp.einsum('tk,tke->et', logit_grad, onehot)
    router_grad = jnp.dot(weights_by_expert, layer_input.astype(jnp.float32), precision=lax.Precision.HIGHEST)
    return hidden_grad, down_grad, logit_grad, router_grad
```

```python
import jax
import jax.numpy as jnp
from jax import lax
from jax.experimental import pallas as pl
from jax.experimental.pallas import tpu as pltpu
from jax.sharding import PartitionSpec as P

BF = jnp.bfloat16
F32 = jnp.float32


def dot(a, b):
    return jnp.dot(a, b, preferred_element_type=F32)


def exact_dot(a, b):
    return jnp.dot(a, b, precision=lax.Precision.HIGHEST, preferred_element_type=F32)


def place_kernel(capacity, ids_ref, logits_ref, rows_ref, send_ref, key_ref, gating_ref):
    top, tokens = ids_ref.shape
    experts = key_ref.shape[0]
    ids = ids_ref[...]
    raised = jnp.exp(logits_ref[...])
    gating = raised / jnp.sum(raised, axis=0, keepdims=True)
    gating_ref[...] = gating
    rounded = gating.astype(BF).astype(F32)
    expert = lax.broadcasted_iota(jnp.int32, (experts, tokens), 0)
    named = jnp.zeros((experts, tokens), F32)
    gate = jnp.zeros((experts, tokens), F32)
    for k in range(top):
        here = ids[k : k + 1, :] == expert
        named = jnp.where(here, 1.0, named)
        gate = jnp.where(here, rounded[k : k + 1, :], gate)
    first = lax.broadcasted_iota(jnp.int32, (tokens, tokens), 0)
    later = lax.broadcasted_iota(jnp.int32, (tokens, tokens), 1)
    before = jnp.where(first < later, 1.0, 0.0).astype(BF)
    slot = dot(named.astype(BF), before)
    key = jnp.where(named > 0.0, slot, -1.0).astype(jnp.int32)
    key_ref[...] = key
    shape = (experts, capacity, tokens)
    slots = lax.broadcasted_iota(jnp.int32, shape, 1)
    chosen = jnp.where(key[:, None, :] == slots, gate[:, None, :], 0.0)
    chosen = chosen.reshape(experts * capacity, tokens).astype(BF)
    send_ref[...] = dot(chosen, rows_ref[...]).astype(BF)


def pick_kernel(back_ref, ids_ref, key_ref, out_ref):
    experts, capacity = back_ref.shape
    top, tokens = ids_ref.shape
    key = key_ref[...]
    back = back_ref[...]
    dense = jnp.zeros((experts, tokens), F32)
    for c in range(capacity):
        dense = jnp.where(key == c, back[:, c : c + 1], dense)
    expert = lax.broadcasted_iota(jnp.int32, (experts, tokens), 0)
    for k in range(top):
        here = ids_ref[k : k + 1, :] == expert
        out_ref[k : k + 1, :] = jnp.sum(jnp.where(here, dense, 0.0), axis=0, keepdims=True)


def grad_kernel(parts_ref, gating_ref, ids_ref, input_ref, logit_ref, term_ref):
    top, tokens = ids_ref.shape
    experts = term_ref.shape[0]
    gating = gating_ref[...]
    total = jnp.sum(parts_ref[...], axis=0)
    delta = total / gating.astype(BF).astype(F32)
    grad = gating * (delta - jnp.sum(gating * delta, axis=0, keepdims=True))
    logit_ref[...] = grad
    expert = lax.broadcasted_iota(jnp.int32, (experts, tokens), 0)
    spread = jnp.zeros((experts, tokens), F32)
    for k in range(top):
        spread = jnp.where(ids_ref[k : k + 1, :] == expert, grad[k : k + 1, :], spread)
    term_ref[...] = exact_dot(spread, input_ref[...].astype(F32))


def whole(shape, dtype):
    return jax.ShapeDtypeStruct(shape, dtype)


def body(
    out_grad, layer_input, expert_ids, selected_logits, saved_hidden, saved_output, down_weight
):
    n_expert = lax.axis_size("expert")
    n_dp = lax.axis_size("dp")
    tokens, top = expert_ids.shape
    dcols = out_grad.shape[1]
    capacity, ff = saved_hidden.shape[2:]
    experts = n_expert
    ids = expert_ids.T
    logits = selected_logits.T
    send, key, gating = pl.pallas_call(
        lambda *refs: place_kernel(capacity, *refs),
        out_shape=(
            whole((experts * capacity, dcols), BF),
            whole((experts, tokens), jnp.int32),
            whole((top, tokens), F32),
        ),
        name="place",
    )(ids, logits, out_grad)
    got = lax.all_to_all(
        send.reshape(n_expert, capacity, dcols), "expert", split_axis=0, concat_axis=0, tiled=True
    )
    outputs = saved_output.reshape(n_expert, capacity, dcols)
    hidden = saved_hidden.reshape(n_expert * capacity, ff)
    weight = down_weight.reshape(dcols, ff)
    back = jnp.sum(got.astype(F32) * outputs.astype(F32), axis=-1)
    by_slot = lax.optimization_barrier(jnp.swapaxes(got, 0, 1))
    part = dot(by_slot.reshape(capacity * n_expert, dcols), weight)
    summed = lax.psum_scatter(
        part.reshape(capacity, n_expert, ff), "dp", scatter_dimension=0, tiled=True
    )
    hidden_grad = jnp.swapaxes(summed, 0, 1).astype(BF).reshape(n_expert, 1, capacity // n_dp, ff)
    down_grad = lax.dot_general(
        got.reshape(n_expert * capacity, dcols),
        hidden,
        (((0,), (0,)), ((), ())),
        preferred_element_type=F32,
    )
    returned = lax.all_to_all(back[:, None, :], "expert", 0, 0, tiled=True)
    picked = pl.pallas_call(pick_kernel, out_shape=whole((top, tokens), F32), name="pick")(
        returned.reshape(n_expert, capacity), ids, key
    )
    copies = jnp.broadcast_to(picked, (n_dp, top, tokens))
    parts = lax.all_to_all(copies, "dp", 0, 0, tiled=True)
    logit_grad, term = pl.pallas_call(
        grad_kernel,
        out_shape=(whole((top, tokens), F32), whole((experts, dcols), F32)),
        name="grads",
    )(parts, gating, ids, layer_input)
    tiles = lax.all_to_all(term.reshape(n_expert, 1, dcols), "expert", 0, 0, tiled=True)
    router_grad = jnp.sum(tiles, axis=0)
    return (hidden_grad, down_grad.reshape(1, dcols, ff), logit_grad.T, router_grad)


def solution(mesh):
    placed = (
        P("expert", "dp"),
        P("expert", "dp"),
        P("expert", None),
        P("expert", None),
        P(None, "expert", None, None),
        P(None, "expert", None, "dp"),
        P("expert", "dp", None),
    )
    return jax.shard_map(
        body,
        mesh=mesh,
        in_specs=placed,
        out_specs=(
            P(None, "expert", "dp", None),
            P("expert", "dp", None),
            P("expert", None),
            P("expert", "dp"),
        ),
        check_vma=False,
    )
```

```python
import jax
import jax.numpy as jnp
from jax import lax
from jax.experimental import pallas as pl
from jax.experimental.pallas import tpu as pltpu
from jax.sharding import PartitionSpec as P


BF = jnp.bfloat16
F32 = jnp.float32


def dot(a, b):
    return jnp.dot(a, b, preferred_element_type=F32)


def exact_dot(a, b):
    return jnp.dot(a, b, precision=lax.Precision.HIGHEST, preferred_element_type=F32)


def place_kernel(capacity, ids_ref, logits_ref, rows_ref, send_ref, key_ref, gating_ref):
    top, tokens = ids_ref.shape
    experts = key_ref.shape[0]
    ids = ids_ref[...]
    raised = jnp.exp(logits_ref[...])
    gating = raised / jnp.sum(raised, axis=0, keepdims=True)
    gating_ref[...] = gating
    rounded = gating.astype(BF).astype(F32)
    expert = lax.broadcasted_iota(jnp.int32, (experts, tokens), 0)
    named = jnp.zeros((experts, tokens), F32)
    gate = jnp.zeros((experts, tokens), F32)
    for k in range(top):
        here = ids[k : k + 1, :] == expert
        named = jnp.where(here, 1.0, named)
        gate = jnp.where(here, rounded[k : k + 1, :], gate)
    first = lax.broadcasted_iota(jnp.int32, (tokens, tokens), 0)
    later = lax.broadcasted_iota(jnp.int32, (tokens, tokens), 1)
    before = jnp.where(first < later, 1.0, 0.0).astype(BF)
    slot = dot(named.astype(BF), before)
    key = jnp.where(named > 0.0, slot, -1.0).astype(jnp.int32)
    key_ref[...] = key
    shape = (experts, capacity, tokens)
    slots = lax.broadcasted_iota(jnp.int32, shape, 1)
    chosen = jnp.where(key[:, None, :] == slots, gate[:, None, :], 0.0)
    chosen = chosen.reshape(experts * capacity, tokens).astype(BF)
    send_ref[...] = dot(chosen, rows_ref[...]).astype(BF)


def turn_kernel(own, me_ref, rows_ref, mine_ref, other_ref):
    capacity = rows_ref.shape[1]
    turned = jnp.swapaxes(rows_ref[...].astype(F32), 0, 1)
    first = me_ref[1] == 0
    for chip in range(capacity // (2 * own)):
        for j in range(own):
            low, high = turned[2 * own * chip + j], turned[2 * own * chip + own + j]
            mine_ref[own * chip + j] = jnp.where(first, low, high).astype(BF)
            other_ref[own * chip + j] = jnp.where(first, high, low).astype(BF)


def hidden_kernel(me_ref, mine_ref, theirs_ref, weight_ref, weights_ref, *out_refs):
    chips = len(out_refs)
    count = out_refs[0].shape[0]
    for d, out_ref in enumerate(out_refs):
        at = pl.ds(lax.rem(me_ref[0] + d, chips) * count, count)
        total = dot(mine_ref[at, :], weight_ref[...]) + dot(theirs_ref[at, :], weights_ref[...])
        out_ref[...] = total.astype(BF)


def sum_kernel(*refs):
    out_ref = refs[-1]
    total = refs[0][...].astype(F32)
    for ref in refs[1:-1]:
        total = total + ref[...].astype(F32)
    sources, own, _ = out_ref.shape
    rows = [total[j * sources : (j + 1) * sources] for j in range(own)]
    out_ref[...] = jnp.stack(rows, axis=1).astype(BF)


def pick_kernel(back_ref, ids_ref, key_ref, out_ref):
    experts, capacity = back_ref.shape
    top, tokens = ids_ref.shape
    key = key_ref[...]
    back = back_ref[...]
    dense = jnp.zeros((experts, tokens), F32)
    for c in range(capacity):
        dense = jnp.where(key == c, back[:, c : c + 1], dense)
    expert = lax.broadcasted_iota(jnp.int32, (experts, tokens), 0)
    for k in range(top):
        here = ids_ref[k : k + 1, :] == expert
        row = jnp.sum(jnp.where(here, dense, 0.0), axis=0, keepdims=True)
        out_ref[:, k : k + 1, :] = jnp.broadcast_to(row[None], (out_ref.shape[0], 1, tokens))


def grad_kernel(parts_ref, gating_ref, ids_ref, input_ref, logit_ref, term_ref):
    top, tokens = ids_ref.shape
    experts = term_ref.shape[0]
    gating = gating_ref[...]
    total = jnp.sum(parts_ref[...], axis=0)
    delta = total / gating.astype(BF).astype(F32)
    grad = gating * (delta - jnp.sum(gating * delta, axis=0, keepdims=True))
    logit_ref[...] = grad
    expert = lax.broadcasted_iota(jnp.int32, (experts, tokens), 0)
    spread = jnp.zeros((experts, tokens), F32)
    for k in range(top):
        spread = jnp.where(ids_ref[k : k + 1, :] == expert, grad[k : k + 1, :], spread)
    term_ref[:, 0, :] = exact_dot(spread, input_ref[...].astype(F32))


def whole(shape, dtype):
    return jax.ShapeDtypeStruct(shape, dtype)


def body(
    out_grad, layer_input, expert_ids, selected_logits, saved_hidden, saved_output, down_weight
):
    n_expert = lax.axis_size("expert")
    n_dp = lax.axis_size("dp")
    tokens, top = expert_ids.shape
    dcols = out_grad.shape[1]
    capacity, ff = saved_hidden.shape[2:]
    experts = n_expert
    ids = expert_ids.T
    logits = selected_logits.T
    send, key, gating = pl.pallas_call(
        lambda *refs: place_kernel(capacity, *refs),
        out_shape=(
            whole((experts * capacity, dcols), BF),
            whole((experts, tokens), jnp.int32),
            whole((top, tokens), F32),
        ),
        name="place",
    )(ids, logits, out_grad)
    got = lax.all_to_all(
        send.reshape(n_expert, capacity, dcols), "expert", split_axis=0, concat_axis=0, tiled=True
    )
    outputs = saved_output.reshape(n_expert, capacity, dcols)
    hidden = saved_hidden.reshape(n_expert * capacity, ff)
    weight = down_weight.reshape(dcols, ff)
    chips = n_dp // 2
    own = capacity // n_dp
    half = chips * own
    partner = [(i, i ^ 1) for i in range(n_dp)]
    at = lax.axis_index("dp")
    me = jnp.stack([at // 2, at % 2])
    weights = lax.ppermute(weight, "dp", partner)
    got, weights = lax.optimization_barrier((got, weights))
    back = jnp.sum(got.astype(F32) * outputs.astype(F32), axis=-1)
    returned = lax.all_to_all(back[:, None, :], "expert", 0, 0, tiled=True)
    step = min(16, n_expert)
    turned = pl.BlockSpec((half, step, dcols), lambda i: (0, i, 0))
    mine, other = pl.pallas_call(
        lambda *refs: turn_kernel(own, *refs),
        grid=(n_expert // step,),
        in_specs=[
            pl.BlockSpec(memory_space=pltpu.SMEM),
            pl.BlockSpec((step, capacity, dcols), lambda i: (i, 0, 0)),
        ],
        out_specs=(turned, turned),
        out_shape=(whole((half, n_expert, dcols), BF),) * 2,
        name="turn",
    )(me, got)
    theirs = lax.ppermute(other, "dp", partner)
    count = own * n_expert
    in_vmem = pl.BlockSpec(memory_space=pltpu.VMEM)
    part = pl.pallas_call(
        hidden_kernel,
        in_specs=[pl.BlockSpec(memory_space=pltpu.SMEM)] + [in_vmem] * 4,
        out_shape=(whole((count, ff), BF),) * chips,
        cost_estimate=pl.CostEstimate(
            flops=4 * chips * count * dcols * ff,
            bytes_accessed=4 * chips * count * ff,
            transcendentals=0,
        ),
        name="hidden",
    )(me, mine.reshape(-1, dcols), theirs.reshape(-1, dcols), weight, weights)
    returned, part = lax.optimization_barrier((returned, part))
    shares = [part[0]]
    for d in range(1, chips):
        shares.append(lax.ppermute(part[d], "dp", [(i, (i + 2 * d) % n_dp) for i in range(n_dp)]))
    hidden_grad = pl.pallas_call(sum_kernel, out_shape=whole((n_expert, own, ff), BF), name="total")(
        *shares
    ).reshape(n_expert, 1, own, ff)
    down_grad = lax.dot_general(
        got.reshape(n_expert * capacity, dcols),
        hidden,
        (((0,), (0,)), ((), ())),
        preferred_element_type=F32,
    )
    copies = pl.pallas_call(pick_kernel, out_shape=whole((n_dp, top, tokens), F32), name="pick")(
        returned.reshape(n_expert, capacity), ids, key
    )
    parts = lax.all_to_all(copies, "dp", 0, 0, tiled=True)
    logit_grad, term = pl.pallas_call(
        grad_kernel,
        out_shape=(whole((top, tokens), F32), whole((experts, 1, dcols), F32)),
        name="grads",
    )(parts, gating, ids, layer_input)
    tiles = lax.all_to_all(term, "expert", 0, 0, tiled=True)
    router_grad = jnp.sum(tiles, axis=0)
    return (hidden_grad, down_grad.reshape(1, dcols, ff), logit_grad.T, router_grad)


def solution(mesh):
    placed = (
        P("expert", "dp"),
        P("expert", "dp"),
        P("expert", None),
        P("expert", None),
        P(None, "expert", None, None),
        P(None, "expert", None, "dp"),
        P("expert", "dp", None),
    )

    return jax.shard_map(
        body,
        mesh=mesh,
        in_specs=placed,
        out_specs=(
            P(None, "expert", "dp", None),
            P("expert", "dp", None),
            P("expert", None),
            P("expert", "dp"),
        ),
        check_vma=False,
    )
```

```python
import jax
import jax.numpy as jnp
from jax import lax
from jax.experimental import pallas as pl
from jax.experimental.pallas import tpu as pltpu
from jax.sharding import PartitionSpec as P


BF = jnp.bfloat16
F32 = jnp.float32


def dot(a, b):
    return jnp.dot(a, b, preferred_element_type=F32)


def exact_dot(a, b):
    return jnp.dot(a, b, precision=lax.Precision.HIGHEST, preferred_element_type=F32)


def place_kernel(capacity, ids_ref, logits_ref, rows_ref, send_ref, key_ref, gating_ref):
    top, tokens = ids_ref.shape
    experts = key_ref.shape[0]
    ids = ids_ref[...]
    raised = jnp.exp(logits_ref[...])
    gating = raised / jnp.sum(raised, axis=0, keepdims=True)
    gating_ref[...] = gating
    rounded = gating.astype(BF).astype(F32)
    expert = lax.broadcasted_iota(jnp.int32, (experts, tokens), 0)
    named = jnp.zeros((experts, tokens), F32)
    gate = jnp.zeros((experts, tokens), F32)
    for k in range(top):
        here = ids[k : k + 1, :] == expert
        named = jnp.where(here, 1.0, named)
        gate = jnp.where(here, rounded[k : k + 1, :], gate)
    first = lax.broadcasted_iota(jnp.int32, (tokens, tokens), 0)
    later = lax.broadcasted_iota(jnp.int32, (tokens, tokens), 1)
    before = jnp.where(first < later, 1.0, 0.0).astype(BF)
    slot = dot(named.astype(BF), before)
    key = jnp.where(named > 0.0, slot, -1.0).astype(jnp.int32)
    key_ref[...] = key
    shape = (experts, capacity, tokens)
    slots = lax.broadcasted_iota(jnp.int32, shape, 1)
    chosen = jnp.where(key[:, None, :] == slots, gate[:, None, :], 0.0)
    chosen = chosen.reshape(experts * capacity, tokens).astype(BF)
    send_ref[...] = dot(chosen, rows_ref[...]).astype(BF)


def turn_kernel(own, me_ref, rows_ref, *refs):
    *out_refs, turned_ref = refs
    members = len(out_refs)
    turned_ref[...] = jnp.swapaxes(rows_ref[...].astype(F32), 0, 1).astype(BF)
    for p, out_ref in enumerate(out_refs):
        member = jnp.bitwise_xor(me_ref[1], p)
        for at in range(out_ref.shape[0]):
            base = (at // own) * members * own + at % own
            out_ref[at] = turned_ref[base + member * own]


def hidden_kernel(members, me_ref, *refs):
    rows_refs, weight_refs = refs[:members], refs[members : 2 * members]
    *out_refs, total_ref = refs[2 * members :]
    total = dot(rows_refs[0][...], weight_refs[0][...])
    for rows_ref, weight_ref in zip(rows_refs[1:], weight_refs[1:]):
        total = total + dot(rows_ref[...], weight_ref[...])
    total_ref[...] = total
    groups = len(out_refs)
    count = out_refs[0].shape[0]
    for d, out_ref in enumerate(out_refs):
        at = pl.ds(pl.multiple_of(lax.rem(me_ref[0] + d, groups) * count, count), count)
        out_ref[...] = total_ref[at, :].astype(BF)


def sum_kernel(*refs):
    out_ref = refs[-1]
    total = refs[0][...].astype(F32)
    for ref in refs[1:-1]:
        total = total + ref[...].astype(F32)
    sources, own, _ = out_ref.shape
    rows = [total[j * sources : (j + 1) * sources] for j in range(own)]
    out_ref[...] = jnp.stack(rows, axis=1).astype(BF)


def pick_kernel(back_ref, ids_ref, key_ref, out_ref):
    experts, capacity = back_ref.shape
    top, tokens = ids_ref.shape
    key = key_ref[...]
    back = back_ref[...]
    dense = jnp.zeros((experts, tokens), F32)
    for c in range(capacity):
        dense = jnp.where(key == c, back[:, c : c + 1], dense)
    expert = lax.broadcasted_iota(jnp.int32, (experts, tokens), 0)
    for k in range(top):
        here = ids_ref[k : k + 1, :] == expert
        row = jnp.sum(jnp.where(here, dense, 0.0), axis=0, keepdims=True)
        out_ref[:, k : k + 1, :] = jnp.broadcast_to(row[None], (out_ref.shape[0], 1, tokens))


def grad_kernel(parts_ref, gating_ref, ids_ref, input_ref, logit_ref, term_ref):
    top, tokens = ids_ref.shape
    experts = term_ref.shape[0]
    gating = gating_ref[...]
    total = jnp.sum(parts_ref[...], axis=0)
    delta = total / gating.astype(BF).astype(F32)
    grad = gating * (delta - jnp.sum(gating * delta, axis=0, keepdims=True))
    logit_ref[...] = grad
    expert = lax.broadcasted_iota(jnp.int32, (experts, tokens), 0)
    spread = jnp.zeros((experts, tokens), F32)
    for k in range(top):
        spread = jnp.where(ids_ref[k : k + 1, :] == expert, grad[k : k + 1, :], spread)
    term_ref[:, 0, :] = exact_dot(spread, input_ref[...].astype(F32))


def whole(shape, dtype):
    return jax.ShapeDtypeStruct(shape, dtype)


def body(
    out_grad, layer_input, expert_ids, selected_logits, saved_hidden, saved_output, down_weight
):
    n_expert = lax.axis_size("expert")
    n_dp = lax.axis_size("dp")
    tokens, top = expert_ids.shape
    dcols = out_grad.shape[1]
    capacity, ff = saved_hidden.shape[2:]
    experts = n_expert
    ids = expert_ids.T
    logits = selected_logits.T
    send, key, gating = pl.pallas_call(
        lambda *refs: place_kernel(capacity, *refs),
        out_shape=(
            whole((experts * capacity, dcols), BF),
            whole((experts, tokens), jnp.int32),
            whole((top, tokens), F32),
        ),
        name="place",
    )(ids, logits, out_grad)
    got = lax.all_to_all(
        send.reshape(n_expert, capacity, dcols), "expert", split_axis=0, concat_axis=0, tiled=True
    )
    outputs = saved_output.reshape(n_expert, capacity, dcols)
    hidden = saved_hidden.reshape(n_expert * capacity, ff)
    weight = down_weight.reshape(dcols, ff)
    members = 4
    groups = n_dp // members
    own = capacity // n_dp
    mine = groups * own
    at = lax.axis_index("dp")
    me = jnp.stack([lax.div(at, members), lax.rem(at, members)])

    def swapped(x, p):
        return lax.ppermute(x, "dp", [(i, i ^ p) for i in range(n_dp)])

    weights = [weight] + [swapped(weight, p) for p in range(1, members)]
    got, weights = lax.optimization_barrier((got, weights))
    back = jnp.sum(got.astype(F32) * outputs.astype(F32), axis=-1)
    returned = lax.all_to_all(back[:, None, :], "expert", 0, 0, tiled=True)
    step = min(16, n_expert)
    turned = pl.BlockSpec((mine, step, dcols), lambda i: (0, i, 0))
    sets = pl.pallas_call(
        lambda *refs: turn_kernel(own, *refs),
        grid=(n_expert // step,),
        in_specs=[
            pl.BlockSpec(memory_space=pltpu.SMEM),
            pl.BlockSpec((step, capacity, dcols), lambda i: (i, 0, 0)),
        ],
        out_specs=(turned,) * members,
        out_shape=(whole((mine, n_expert, dcols), BF),) * members,
        scratch_shapes=[pltpu.VMEM((capacity, step, dcols), BF)],
        name="turn",
    )(me, got)
    rows = [sets[0]] + [swapped(sets[p], p) for p in range(1, members)]
    count = own * n_expert
    in_vmem = pl.BlockSpec(memory_space=pltpu.VMEM)
    part = pl.pallas_call(
        lambda *refs: hidden_kernel(members, *refs),
        in_specs=[pl.BlockSpec(memory_space=pltpu.SMEM)] + [in_vmem] * (2 * members),
        out_shape=(whole((count, ff), BF),) * groups,
        scratch_shapes=[pltpu.VMEM((groups * count, ff), F32)],
        cost_estimate=pl.CostEstimate(
            flops=2 * members * groups * count * dcols * ff,
            bytes_accessed=4 * groups * count * ff,
            transcendentals=0,
        ),
        name="hidden",
    )(me, *[r.reshape(-1, dcols) for r in rows], *weights)
    shares = [part[0]]
    for d in range(1, groups):
        shares.append(
            lax.ppermute(part[d], "dp", [(i, (i + members * d) % n_dp) for i in range(n_dp)])
        )
    hidden_grad = pl.pallas_call(sum_kernel, out_shape=whole((n_expert, own, ff), BF), name="total")(
        *shares
    ).reshape(n_expert, 1, own, ff)
    down_grad = lax.dot_general(
        got.reshape(n_expert * capacity, dcols),
        hidden,
        (((0,), (0,)), ((), ())),
        preferred_element_type=F32,
    )
    copies = pl.pallas_call(pick_kernel, out_shape=whole((n_dp, top, tokens), F32), name="pick")(
        returned.reshape(n_expert, capacity), ids, key
    )
    parts = lax.all_to_all(copies, "dp", 0, 0, tiled=True)
    logit_grad, term = pl.pallas_call(
        grad_kernel,
        out_shape=(whole((top, tokens), F32), whole((experts, 1, dcols), F32)),
        name="grads",
    )(parts, gating, ids, layer_input)
    tiles = lax.all_to_all(term, "expert", 0, 0, tiled=True)
    router_grad = jnp.sum(tiles, axis=0)
    return (hidden_grad, down_grad.reshape(1, dcols, ff), logit_grad.T, router_grad)


def solution(mesh):
    placed = (
        P("expert", "dp"),
        P("expert", "dp"),
        P("expert", None),
        P("expert", None),
        P(None, "expert", None, None),
        P(None, "expert", None, "dp"),
        P("expert", "dp", None),
    )

    return jax.shard_map(
        body,
        mesh=mesh,
        in_specs=placed,
        out_specs=(
            P(None, "expert", "dp", None),
            P("expert", "dp", None),
            P("expert", None),
            P("expert", "dp"),
        ),
        check_vma=False,
    )
```

```python
import jax
import jax.numpy as jnp
from jax import lax
from jax.experimental import pallas as pl
from jax.experimental.pallas import tpu as pltpu
from jax.sharding import PartitionSpec as P


BF = jnp.bfloat16
F32 = jnp.float32


def dot(a, b):
    return jnp.dot(a, b, preferred_element_type=F32)


def exact_dot(a, b):
    return jnp.dot(a, b, precision=lax.Precision.HIGHEST, preferred_element_type=F32)


def place_kernel(capacity, ids_ref, logits_ref, rows_ref, send_ref, key_ref, gating_ref):
    top, tokens = ids_ref.shape
    experts = key_ref.shape[0]
    ids = ids_ref[...]
    raised = jnp.exp(logits_ref[...])
    gating = raised / jnp.sum(raised, axis=0, keepdims=True)
    gating_ref[...] = gating
    rounded = gating.astype(BF).astype(F32)
    expert = lax.broadcasted_iota(jnp.int32, (experts, tokens), 0)
    named = jnp.zeros((experts, tokens), F32)
    gate = jnp.zeros((experts, tokens), F32)
    for k in range(top):
        here = ids[k : k + 1, :] == expert
        named = jnp.where(here, 1.0, named)
        gate = jnp.where(here, rounded[k : k + 1, :], gate)
    first = lax.broadcasted_iota(jnp.int32, (tokens, tokens), 0)
    later = lax.broadcasted_iota(jnp.int32, (tokens, tokens), 1)
    before = jnp.where(first < later, 1.0, 0.0).astype(BF)
    slot = dot(named.astype(BF), before)
    key = jnp.where(named > 0.0, slot, -1.0).astype(jnp.int32)
    key_ref[...] = key
    shape = (experts, capacity, tokens)
    slots = lax.broadcasted_iota(jnp.int32, shape, 1)
    chosen = jnp.where(key[:, None, :] == slots, gate[:, None, :], 0.0)
    chosen = chosen.reshape(experts * capacity, tokens).astype(BF)
    send_ref[...] = dot(chosen, rows_ref[...]).astype(BF)


def turn_kernel(own, me_ref, rows_ref, *refs):
    *out_refs, turned_ref = refs
    members = len(out_refs)
    turned_ref[...] = jnp.swapaxes(rows_ref[...].astype(F32), 0, 1).astype(BF)
    for p, out_ref in enumerate(out_refs):
        member = jnp.bitwise_xor(me_ref[1], p)
        for at in range(out_ref.shape[0]):
            base = (at // own) * members * own + at % own
            out_ref[at] = turned_ref[base + member * own]


def hidden_kernel(members, me_ref, *refs):
    rows_refs, weight_refs = refs[:members], refs[members : 2 * members]
    *out_refs, total_ref = refs[2 * members :]
    total = dot(rows_refs[0][...], weight_refs[0][...])
    for rows_ref, weight_ref in zip(rows_refs[1:], weight_refs[1:]):
        total = total + dot(rows_ref[...], weight_ref[...])
    total_ref[...] = total
    groups = len(out_refs)
    count = out_refs[0].shape[0]
    for d, out_ref in enumerate(out_refs):
        at = pl.ds(pl.multiple_of(lax.rem(me_ref[0] + d, groups) * count, count), count)
        out_ref[...] = total_ref[at, :].astype(BF)


def sum_kernel(*refs):
    out_ref = refs[-1]
    total = refs[0][...].astype(F32)
    for ref in refs[1:-1]:
        total = total + ref[...].astype(F32)
    sources, own, _ = out_ref.shape
    rows = [total[j * sources : (j + 1) * sources] for j in range(own)]
    out_ref[...] = jnp.stack(rows, axis=1).astype(BF)


def pick_kernel(back_ref, ids_ref, key_ref, out_ref):
    experts, capacity = back_ref.shape
    top, tokens = ids_ref.shape
    key = key_ref[...]
    back = back_ref[...]
    dense = jnp.zeros((experts, tokens), F32)
    for c in range(capacity):
        dense = jnp.where(key == c, back[:, c : c + 1], dense)
    expert = lax.broadcasted_iota(jnp.int32, (experts, tokens), 0)
    for k in range(top):
        here = ids_ref[k : k + 1, :] == expert
        row = jnp.sum(jnp.where(here, dense, 0.0), axis=0, keepdims=True)
        out_ref[:, k : k + 1, :] = jnp.broadcast_to(row[None], (out_ref.shape[0], 1, tokens))


def grad_kernel(parts_ref, gating_ref, ids_ref, input_ref, logit_ref, term_ref):
    top, tokens = ids_ref.shape
    experts = term_ref.shape[0]
    gating = gating_ref[...]
    total = jnp.sum(parts_ref[...], axis=0)
    delta = total / gating.astype(BF).astype(F32)
    grad = gating * (delta - jnp.sum(gating * delta, axis=0, keepdims=True))
    logit_ref[...] = grad
    expert = lax.broadcasted_iota(jnp.int32, (experts, tokens), 0)
    spread = jnp.zeros((experts, tokens), F32)
    for k in range(top):
        spread = jnp.where(ids_ref[k : k + 1, :] == expert, grad[k : k + 1, :], spread)
    term_ref[...] = exact_dot(spread, input_ref[...].astype(F32))


def whole(shape, dtype):
    return jax.ShapeDtypeStruct(shape, dtype)


def body(
    out_grad, layer_input, expert_ids, selected_logits, saved_hidden, saved_output, down_weight
):
    n_expert = lax.axis_size("expert")
    n_dp = lax.axis_size("dp")
    tokens, top = expert_ids.shape
    dcols = out_grad.shape[1]
    capacity, ff = saved_hidden.shape[2:]
    experts = n_expert
    ids = expert_ids.T
    logits = selected_logits.T
    send, key, gating = pl.pallas_call(
        lambda *refs: place_kernel(capacity, *refs),
        out_shape=(
            whole((experts * capacity, dcols), BF),
            whole((experts, tokens), jnp.int32),
            whole((top, tokens), F32),
        ),
        name="place",
    )(ids, logits, out_grad)
    got = lax.all_to_all(
        send.reshape(n_expert, capacity, dcols), "expert", split_axis=0, concat_axis=0, tiled=True
    )
    outputs = saved_output.reshape(n_expert, capacity, dcols)
    hidden = saved_hidden.reshape(n_expert * capacity, ff)
    weight = down_weight.reshape(dcols, ff)
    members = 4
    groups = n_dp // members
    own = capacity // n_dp
    mine = groups * own
    at = lax.axis_index("dp")
    me = jnp.stack([lax.div(at, members), lax.rem(at, members)])

    def swapped(x, p):
        return lax.ppermute(x, "dp", [(i, i ^ p) for i in range(n_dp)])

    weights = [weight] + [swapped(weight, p) for p in range(1, members)]
    got, weights = lax.optimization_barrier((got, weights))
    back = jnp.sum(got.astype(F32) * outputs.astype(F32), axis=-1)
    returned = lax.all_to_all(back[:, None, :], "expert", 0, 0, tiled=True)
    step = min(16, n_expert)
    turned = pl.BlockSpec((mine, step, dcols), lambda i: (0, i, 0))
    sets = pl.pallas_call(
        lambda *refs: turn_kernel(own, *refs),
        grid=(n_expert // step,),
        in_specs=[
            pl.BlockSpec(memory_space=pltpu.SMEM),
            pl.BlockSpec((step, capacity, dcols), lambda i: (i, 0, 0)),
        ],
        out_specs=(turned,) * members,
        out_shape=(whole((mine, n_expert, dcols), BF),) * members,
        scratch_shapes=[pltpu.VMEM((capacity, step, dcols), BF)],
        name="turn",
    )(me, got)
    rows = [sets[0]] + [swapped(sets[p], p) for p in range(1, members)]
    count = own * n_expert
    in_vmem = pl.BlockSpec(memory_space=pltpu.VMEM)
    part = pl.pallas_call(
        lambda *refs: hidden_kernel(members, *refs),
        in_specs=[pl.BlockSpec(memory_space=pltpu.SMEM)] + [in_vmem] * (2 * members),
        out_shape=(whole((count, ff), BF),) * groups,
        scratch_shapes=[pltpu.VMEM((groups * count, ff), F32)],
        cost_estimate=pl.CostEstimate(
            flops=2 * members * groups * count * dcols * ff,
            bytes_accessed=4 * groups * count * ff,
            transcendentals=0,
        ),
        name="hidden",
    )(me, *[r.reshape(-1, dcols) for r in rows], *weights)
    shares = [part[0]]
    for d in range(1, groups):
        shares.append(
            lax.ppermute(part[d], "dp", [(i, (i + members * d) % n_dp) for i in range(n_dp)])
        )
    hidden_grad = pl.pallas_call(sum_kernel, out_shape=whole((n_expert, own, ff), BF), name="total")(
        *shares
    ).reshape(n_expert, 1, own, ff)
    down_grad = lax.dot_general(
        got.reshape(n_expert * capacity, dcols),
        hidden,
        (((0,), (0,)), ((), ())),
        preferred_element_type=F32,
    )
    copies = pl.pallas_call(pick_kernel, out_shape=whole((n_dp, top, tokens), F32), name="pick")(
        returned.reshape(n_expert, capacity), ids, key
    )
    parts = lax.all_to_all(copies, "dp", 0, 0, tiled=True)
    logit_grad, term = pl.pallas_call(
        grad_kernel,
        out_shape=(whole((top, tokens), F32), whole((experts, dcols), F32)),
        name="grads",
    )(parts, gating, ids, layer_input)
    tiles = lax.all_to_all(term.reshape(n_expert, 1, dcols), "expert", 0, 0, tiled=True)
    router_grad = jnp.sum(tiles, axis=0)
    return (hidden_grad, down_grad.reshape(1, dcols, ff), logit_grad.T, router_grad)


def solution(mesh):
    placed = (
        P("expert", "dp"),
        P("expert", "dp"),
        P("expert", None),
        P("expert", None),
        P(None, "expert", None, None),
        P(None, "expert", None, "dp"),
        P("expert", "dp", None),
    )

    return jax.shard_map(
        body,
        mesh=mesh,
        in_specs=placed,
        out_specs=(
            P(None, "expert", "dp", None),
            P("expert", "dp", None),
            P("expert", None),
            P("expert", "dp"),
        ),
        check_vma=False,
    )
```
